32 devices in a mesh: dp: 4 (over z), row: 4 (over y, x), col: 2 (over core).
Axes of the slice: x: 2, y: 2, z: 4, core: 2. Of those that a mesh axis runs over, the one named last changes fastest.
Arguments:
- layer_input: bfloat16 [1024, 1024], P('dp', ('row', 'col')), may hold values from -6 to 6
- doc_lengths: int32 [4, 8], P('dp'), may hold values from 1 to 128, 256 in all within a row
- qkv_weight: bfloat16 [1024, 3072], P('row', 'col'), may hold values from -0.1875 to 0.1875
- query_bias: bfloat16 [1024], P(('col', 'row')), may hold values from -3 to 3
- value_bias: bfloat16 [1024], P(('col', 'row')), may hold values from -3 to 3
- out_weight: bfloat16 [1024, 1024], P('col', 'row'), may hold values from -0.75 to 0.75
- out_bias: bfloat16 [1024], P(('row', 'col')), may hold values from -3 to 3
- first_gain: bfloat16 [1024], P(('row', 'col')), may hold values from 0.099609375 to 1.8984375
- first_shift: bfloat16 [1024], P(('row', 'col')), may hold values from -3 to 3
- up_weight: bfloat16 [1024, 4096], P('row', 'col'), may hold values from -0.1875 to 0.1875
- up_bias: bfloat16 [4096], P(('col', 'row')), may hold values from -3 to 3
- down_weight: bfloat16 [4096, 1024], P('col', 'row'), may hold values from -0.09375 to 0.09375
- down_bias: bfloat16 [1024], P(('row', 'col')), may hold values from -3 to 3
- second_gain: bfloat16 [1024], P(('row', 'col')), may hold values from 0.099609375 to 1.8984375
- second_shift: bfloat16 [1024], P(('row', 'col')), may hold values from -3 to 3
- cotangent: float32 [1024, 1024], P('dp', ('row', 'col')), may hold values from -6 to 6
Outputs:
- layer_output: float32 [1024, 1024], P('dp', ('row', 'col'))
- input_grad: float32 [1024, 1024], P('dp', ('row', 'col'))
- qkv_weight_grad: float32 [1024, 3072], P(('row', 'dp'), 'col')
- query_bias_grad: float32 [1024], P(('col', 'row', 'dp'))
- value_bias_grad: float32 [1024], P(('col', 'row', 'dp'))
- out_weight_grad: float32 [1024, 1024], P(('col', 'dp'), 'row')
- out_bias_grad: float32 [1024], P(('row', 'col', 'dp'))
- first_gain_grad: float32 [1024], P(('row', 'col', 'dp'))
- first_shift_grad: float32 [1024], P(('row', 'col', 'dp'))
- up_weight_grad: float32 [1024, 4096], P(('row', 'dp'), 'col')
- up_bias_grad: float32 [4096], P(('col', 'row', 'dp'))
- down_weight_grad: float32 [4096, 1024], P(('col', 'dp'), 'row')
- down_bias_grad: float32 [1024], P(('row', 'col', 'dp'))
- second_gain_grad: float32 [1024], P(('row', 'col', 'dp'))
- second_shift_grad: float32 [1024], P(('row', 'col', 'dp'))
The draws below stay inside these ranges and needn't reach their ends.
Inputs may be any that keep to these rules, and one draw needn't show every extreme that they name: `doc_lengths`: each row lists the lengths of the 8 documents packed in order into one data group; a row sums to 256.
All inputs are finite; a program needn't handle non-finite values.
Results may differ from the reference program's by a relative error of at most 0.014.
Values may be sent and summed in bfloat16 or wider, within the bound.
No kernel may reach another device: no remote copies, remote signals or barrier semaphores. Data moves between devices by JAX's collectives and lax.ppermute only.
A program may use at most 64 MiB of HBM per device.

```python
import math
import jax
import jax.numpy as jnp
import numpy as np
from jax import lax

D = 1024
HEADS = 16
HEAD_DIM = 64
FF = 4096
TOK_G = 256
DOCS = 8
TOKENS = 1024
N_DP = 4


def level_of(rng, extent, pieces, low, high):
    factor_of, own = 1.0, jax.random.fold_in(rng, 6)
    for dim, parts in pieces:
        steps = jnp.exp(jax.random.uniform(jax.random.fold_in(own, dim), (parts,), jnp.float32, low / len(pieces), high / len(pieces)))
        factor_of = factor_of * jnp.repeat(steps, extent[dim] // parts).reshape([-1 if axis == dim else 1 for axis in range(len(extent))])
    return factor_of


def length_profile(amount, total, bound, lean):
    portions = [(1 << 20) // math.isqrt(standing ** lean) + 1 for standing in range(2, amount + 1)]
    spare, given = total - bound - (amount - 1), [1] * (amount - 1)
    while spare > 0:
        movable = [i for i in range(amount - 1) if given[i] < bound]
        mass, budget = sum([portions[i] for i in movable]), spare
        for i in movable:
            addition = min(bound - given[i], max(1, budget * portions[i] // mass), spare)
            given[i] = given[i] + addition
            spare = spare - addition
    return np.array([bound] + given)


def ragged_sizes(key, count, total, bound, slope):
    if count == 2:
        one = jax.random.randint(key, (), max(1, total - bound), min(bound, total - 1) + 1)
        return jnp.stack([one, total - one])
    tallies = jnp.asarray(length_profile(count, total, bound, slope), jnp.int32)
    pairs = (count - 1) // 2
    source_of, sink = tallies[1:1 + 2 * pairs:2], tallies[2:2 + 2 * pairs:2]
    slack = jnp.minimum(source_of - 1, bound - sink)
    passed = jax.random.randint(jax.random.fold_in(key, 1), (pairs,), 0, 1 << 20) % (slack + 1)
    tallies = tallies.at[1:1 + 2 * pairs:2].set(source_of - passed).at[2:2 + 2 * pairs:2].set(sink + passed)
    return tallies[jax.random.permutation(jax.random.fold_in(key, 2), count)]


def normal_values(stream_key, extent, deviation, limit, pieces=(), dtype=jnp.bfloat16):
    loudness = level_of(stream_key, extent, pieces, -0.22, 0.18) if pieces else 1.0
    drawn = jax.random.normal(stream_key, extent, jnp.float32) * deviation * loudness
    return jnp.minimum(jnp.maximum(drawn, -limit), limit).astype(dtype)


def setup_inputs(seed: int = 0) -> dict:
    key_of = jax.random.split(jax.random.key(seed), 17)
    return {
        "layer_input": normal_values(key_of[0], (TOKENS, D), 1.0, 6.0, ((0, 4), (1, 8))),
        "doc_lengths": jax.vmap(lambda own: ragged_sizes(own, DOCS, TOK_G, min(512, TOK_G // 2), 2))(jax.random.split(key_of[1], N_DP)).reshape((N_DP, DOCS)).astype(jnp.int32),
        "qkv_weight": normal_values(key_of[2], (D, 3 * D), D ** -0.5, 0.1875, ((0, 4), (1, 2))),
        "query_bias": normal_values(key_of[3], (D,), 0.5, 3.0, ((0, 8),)),
        "value_bias": normal_values(key_of[4], (D,), 0.5, 3.0, ((0, 8),)),
        "out_weight": normal_values(key_of[5], (D, D), (D // 16) ** -0.5, 0.75, ((0, 2), (1, 4))),
        "out_bias": normal_values(key_of[6], (D,), 0.5, 3.0, ((0, 8),)),
        "first_gain": jnp.clip(1.0 + 0.18 * jax.random.normal(key_of[7], (D,), jnp.float32), 0.099609375, 1.8984375).astype(jnp.bfloat16),
        "first_shift": normal_values(key_of[8], (D,), 0.5, 3.0, ((0, 8),)),
        "up_weight": normal_values(key_of[9], (D, FF), D ** -0.5, 0.1875, ((0, 4), (1, 2))),
        "up_bias": normal_values(key_of[10], (FF,), 0.5, 3.0, ((0, 8),)),
        "down_weight": normal_values(key_of[11], (FF, D), FF ** -0.5, 0.09375, ((0, 2), (1, 4))),
        "down_bias": normal_values(key_of[12], (D,), 0.5, 3.0, ((0, 8),)),
        "second_gain": jnp.clip(1.0 + 0.18 * jax.random.normal(key_of[13], (D,), jnp.float32), 0.099609375, 1.8984375).astype(jnp.bfloat16),
        "second_shift": normal_values(key_of[14], (D,), 0.5, 3.0, ((0, 8),)),
        "cotangent": normal_values(key_of[15], (TOKENS, D), 1.0, 6.0, ((0, 4), (1, 8)), jnp.float32),
    }


EPSILON = 1e-12

def matmul(left, right):
    return jnp.dot(left, right, preferred_element_type=jnp.float32)

def matmul_transposed(left, right):
    return lax.dot_general(left, right, (((1,), (1,)), ((), ())), preferred_element_type=jnp.float32)

def outer_product(left, right):
    return lax.dot_general(left, right, (((0,), (0,)), ((), ())), preferred_element_type=jnp.float32)

def gelu_value(pre):
    return 0.5 * pre * (1.0 + jax.scipy.special.erf(pre / math.sqrt(2.0)))

def gelu_slope(pre):
    return 0.5 * (1.0 + jax.scipy.special.erf(pre / math.sqrt(2.0))) + pre * jnp.exp(-0.5 * pre * pre) / math.sqrt(2.0 * math.pi)

def norm_forward(resid, norm_gain, norm_shift):
    row_mean = lax.optimization_barrier(jnp.mean(resid, -1, keepdims=True))
    centred = resid - row_mean
    variance = lax.optimization_barrier(jnp.mean(centred * centred, -1, keepdims=True))
    inv_std = lax.rsqrt(variance + EPSILON)
    normed = centred * inv_std
    return (normed * norm_gain + norm_shift, normed, inv_std)

def norm_backward(upstream, normed, inv_std, norm_gain):
    scaled = upstream * norm_gain
    first_mean = lax.optimization_barrier(jnp.mean(scaled, -1, keepdims=True))
    second_mean = lax.optimization_barrier(jnp.mean(scaled * normed, -1, keepdims=True))
    result = inv_std * (scaled - first_mean - normed * second_mean)
    return (result, lax.optimization_barrier(jnp.sum(upstream * normed, 0)), lax.optimization_barrier(jnp.sum(upstream, 0)))

def reference(layer_input, doc_lengths, qkv_weight, query_bias, value_bias, out_weight, out_bias, first_gain, first_shift, up_weight, up_bias, down_weight, down_bias, second_gain, second_shift, cotangent):
    bfloat = jnp.bfloat16
    single = jnp.float32
    score_scale = 1.0 / math.sqrt(HEAD_DIM)
    gain_one = first_gain.astype(single)
    shift_one = first_shift.astype(single)
    gain_two = second_gain.astype(single)
    shift_two = second_shift.astype(single)

    def one_group(running, group_items):
        inputs, doc_row, upstream_out = group_items
        doc_ends = jnp.cumsum(doc_row)
        position = jnp.arange(TOK_G).astype(jnp.int32)
        segment = lax.optimization_barrier(jnp.sum((position[:, None] >= doc_ends[None, :]).astype(jnp.int32), 1))
        same_doc = (segment[:, None] == segment[None, :])[None]
        qkv = matmul(inputs, qkv_weight).reshape(TOK_G, HEADS, 3, HEAD_DIM)
        queries = (qkv[:, :, 0] + query_bias.astype(single).reshape(HEADS, HEAD_DIM)).astype(bfloat)
        keys = qkv[:, :, 1].astype(bfloat)
        values = (qkv[:, :, 2] + value_bias.astype(single).reshape(HEADS, HEAD_DIM)).astype(bfloat)
        scores = jnp.einsum('qhe,khe->hqk', queries.astype(single), keys.astype(single)) * score_scale
        scores = jnp.where(same_doc, scores, -1e+30)
        top_score = lax.optimization_barrier(jnp.max(scores, -1, keepdims=True))
        logsum = top_score + jnp.log(lax.optimization_barrier(jnp.sum(jnp.exp(scores - top_score), -1, keepdims=True)))
        probabilities = jnp.exp(scores - logsum)
        prob_bf = probabilities.astype(bfloat)
        context = jnp.einsum('hqk,khe->qhe', prob_bf.astype(single), values.astype(single))
        context = context.astype(bfloat).reshape(TOK_G, D)
        resid_one = matmul(context, out_weight) + out_bias.astype(single) + inputs.astype(single)
        hidden_one, normed_one, inv_one = norm_forward(resid_one, gain_one, shift_one)
        hidden_bf = hidden_one.astype(bfloat)
        pre_act = matmul(hidden_bf, up_weight) + up_bias.astype(single)
        activated = gelu_value(pre_act).astype(bfloat)
        resid_two = matmul(activated, down_weight) + down_bias.astype(single) + hidden_one
        output, normed_two, inv_two = norm_forward(resid_two, gain_two, shift_two)
        grad_two, gain_two_grad, shift_two_grad = norm_backward(upstream_out, normed_two, inv_two, gain_two)
        grad_two_bf = grad_two.astype(bfloat)
        down_weight_grad = outer_product(activated, grad_two_bf)
        grad_pre = matmul_transposed(grad_two_bf, down_weight) * gelu_slope(pre_act)
        grad_pre_bf = grad_pre.astype(bfloat)
        up_weight_grad = outer_product(hidden_bf, grad_pre_bf)
        grad_hidden = grad_two + matmul_transposed(grad_pre_bf, up_weight)
        grad_one, gain_one_grad, shift_one_grad = norm_backward(grad_hidden, normed_one, inv_one, gain_one)
        grad_one_bf = grad_one.astype(bfloat)
        out_weight_grad = outer_product(context, grad_one_bf)
        grad_context = matmul_transposed(grad_one_bf, out_weight).astype(bfloat).reshape(TOK_G, HEADS, HEAD_DIM)
        grad_probs = jnp.einsum('qhe,khe->hqk', grad_context.astype(single), values.astype(single))
        row_dot = lax.optimization_barrier(jnp.sum(probabilities * grad_probs, -1, keepdims=True))
        grad_scores = (probabilities * (grad_probs - row_dot)).astype(bfloat)
        query_grad = jnp.einsum('hqk,khe->qhe', grad_scores.astype(single), keys.astype(single)) * score_scale
        key_grad = jnp.einsum('hqk,qhe->khe', grad_scores.astype(single), queries.astype(single)) * score_scale
        value_grad = jnp.einsum('hqk,qhe->khe', prob_bf.astype(single), grad_context.astype(single))
        grad_qkv = jnp.stack([query_grad, key_grad, value_grad], 2).reshape(TOK_G, 3 * D).astype(bfloat)
        qkv_weight_grad = outer_product(inputs, grad_qkv)
        input_grad = grad_one + matmul_transposed(grad_qkv, qkv_weight)
        terms = (qkv_weight_grad, lax.optimization_barrier(jnp.sum(query_grad, 0)).reshape(D), lax.optimization_barrier(jnp.sum(value_grad, 0)).reshape(D), out_weight_grad, lax.optimization_barrier(jnp.sum(grad_one, 0)), gain_one_grad, shift_one_grad, up_weight_grad, lax.optimization_barrier(jnp.sum(grad_pre, 0)), down_weight_grad, lax.optimization_barrier(jnp.sum(grad_two, 0)), gain_two_grad, shift_two_grad)
        running = jax.tree.map(lambda first, second: first + second, running, terms)
        return (running, (output, input_grad))
    initial = (jnp.zeros((D, 3 * D), single), jnp.zeros((D,), single), jnp.zeros((D,), single), jnp.zeros((D, D), single), jnp.zeros((D,), single), jnp.zeros((D,), single), jnp.zeros((D,), single), jnp.zeros((D, FF), single), jnp.zeros((FF,), single), jnp.zeros((FF, D), single), jnp.zeros((D,), single), jnp.zeros((D,), single), jnp.zeros((D,), single))
    group_inputs = (layer_input.reshape(N_DP, TOK_G, D), doc_lengths, cotangent.reshape(N_DP, TOK_G, D).astype(single))
    running, (outputs, grads_in) = lax.scan(one_group, initial, group_inputs)
    return (outputs.reshape(N_DP * TOK_G, D), grads_in.reshape(N_DP * TOK_G, D), running[0], running[1], running[2], running[3], running[4], running[5], running[6], running[7], running[8], running[9], running[10], running[11], running[12])
```

```python
import functools
import math

import jax
import jax.numpy as jnp
from jax import lax
from jax.experimental import pallas as pl
from jax.experimental.pallas import tpu as pltpu
from jax.sharding import PartitionSpec as P

HEAD_DIM = 64
EPSILON = 1e-12
BF = jnp.bfloat16
F32 = jnp.float32


def dot(left, right):
    return lax.dot_general(left, right, (((1,), (0,)), ((), ())), preferred_element_type=F32)


def dot_nt(left, right):
    return lax.dot_general(left, right, (((1,), (1,)), ((), ())), preferred_element_type=F32)


def dot_tn(left, right):
    return lax.dot_general(left, right, (((0,), (0,)), ((), ())), preferred_element_type=F32)


def call(body, outs, *args, scratch=(), flops=0, smem=()):
    moved = sum(a.size * a.dtype.itemsize for a in args)
    moved += sum(math.prod(s) * jnp.dtype(d).itemsize for s, d in outs)
    space = [pltpu.SMEM if i in smem else pltpu.VMEM for i in range(len(args))]
    return pl.pallas_call(
        body,
        out_shape=[jax.ShapeDtypeStruct(s, d) for s, d in outs],
        in_specs=[pl.BlockSpec(memory_space=m) for m in space],
        out_specs=[pl.BlockSpec(memory_space=pltpu.VMEM) for _ in outs],
        scratch_shapes=[pltpu.VMEM(s, d) for s, d in scratch],
        compiler_params=pltpu.CompilerParams(vmem_limit_bytes=48 << 20),
        cost_estimate=pl.CostEstimate(flops=flops, bytes_accessed=moved, transcendentals=0),
    )(*args)


def lanes(index, width):
    return pl.ds(pl.multiple_of(index * width, width), width)


def row_mean(x):
    return jnp.sum(x, 1, keepdims=True) / x.shape[1]


def fast_local(
    layer_input, doc_lengths, qkv_weight, query_bias, value_bias, out_weight, out_bias,
    first_gain, first_shift, up_weight, up_bias, down_weight, down_bias, second_gain,
    second_shift, cotangent,
):
    R, C, Z = (lax.axis_size(name) for name in ("row", "col", "dp"))
    T, DB = layer_input.shape
    TH, TQ = T // C, T // C // 2
    KR, D = DB * C, DB * C * R
    HD = query_bias.shape[0]
    HEADS = HD // HEAD_DIM
    Q3 = 3 * HD
    F8 = up_bias.shape[0]
    FW = F8 // Z
    NU = F8 // KR
    OP = KR // HD
    DOCS = doc_lengths.shape[1]
    ZB = KR // Z
    scale = 1.0 / math.sqrt(HEAD_DIM)
    VB = F8 // DB

    def prow(x, k):
        return lax.ppermute(x, "row", [(i, i ^ k) for i in range(R)])

    def pcol(x):
        return lax.ppermute(x, "col", [(i, C - 1 - i) for i in range(C)])

    def pz(x, k):
        return lax.ppermute(x, "dp", [(i, i ^ k) for i in range(Z)])

    def phop(x, second):
        pairs = []
        for r in range(R):
            for c in range(C):
                mask = 1 << ((c + second) % 2)
                pairs.append((r * C + c, (r ^ mask) * C + c))
        return lax.ppermute(x, ("row", "col"), pairs)

    def here():
        return lax.axis_index("row"), lax.axis_index("col"), lax.axis_index("dp")

    others = range(1, R)

    def pack_a(wq, wo, *outs):
        r, _, _ = here()
        for k in range(R):
            d = r ^ k
            outs[k][:, :Q3] = wq[:, lanes(d, Q3)]
            piece = wo[lanes(d, HD), :]
            for i in range(OP):
                outs[k][i * HD : (i + 1) * HD, Q3:] = piece[:, i * HD : (i + 1) * HD]

    def pack_x(x, vec, out):
        out[:T] = x[...]
        out[T:] = vec[...]

    vecs = [out_bias, first_gain, first_shift, down_bias, second_gain, second_shift]
    vec = jnp.concatenate([v.reshape(1, DB) for v in vecs] + [up_bias.reshape(VB, DB)], 0)
    vec = jnp.pad(vec, ((0, 16 - vec.shape[0]), (0, 0)))
    A = call(pack_a, [((KR, Q3 + HD), BF)] * R, qkv_weight, out_weight)
    A = [A[0]] + [prow(A[k], k) for k in others]
    (xp,) = call(pack_x, [((T + 16, DB), BF)], layer_input, vec)
    X = [xp] + [prow(xp, k) for k in others]
    Y = [pcol(x) for x in X]

    def pack_b(up, down, *outs):
        r, _, _ = here()
        for k in range(R):
            d = r ^ k
            for zb in range(Z):
                half, off = (zb * FW) // KR, (zb * FW) % KR
                outs[k][half * KR : (half + 1) * KR, off : off + FW] = up[:, lanes(zb * R + d, FW)]
                outs[k][F8 + zb * FW : F8 + (zb + 1) * FW, :] = down[lanes(zb * R + d, FW), :]

    B = call(pack_b, [((2 * F8, KR), BF)] * R, up_weight, down_weight)
    tied = lax.optimization_barrier((tuple(B), tuple(X[1:])))
    B, X = list(tied[0]), [xp] + list(tied[1])
    B = [B[0]] + [prow(B[k], k) for k in others]
    PB = [pcol(b) for b in B]

    def attention(*refs):
        xs, ys, ws = refs[:R], refs[R : 2 * R], refs[2 * R : 3 * R]
        qb, vb, docs, xf, vall, qkv_o, prob_o, ctx_o, p_own, p_send, scr = refs[3 * R :]
        r, c, _ = here()
        for k in range(R):
            for src, cc in ((xs[k], c), (ys[k], C - 1 - c)):
                at = (r ^ k) * C + cc
                xf[:, lanes(at, DB)] = src[:T]
                vall[pl.ds(at, 1)] = src[T:].astype(F32)[None]
        acc = jnp.zeros((T, Q3), F32)
        for k in range(R):
            acc += dot(xf[:, lanes(r ^ k, KR)], ws[k][:, :Q3])
        ends, end = [], 0
        for j in range(DOCS):
            end = end + docs[0, j]
            ends.append(end)
        rows = lax.broadcasted_iota(jnp.int32, (T, 1), 0)
        cols = lax.broadcasted_iota(jnp.int32, (1, T), 1)
        seg_r, seg_c = jnp.zeros((T, 1), jnp.int32), jnp.zeros((1, T), jnp.int32)
        for end in ends:
            seg_r += (rows >= end).astype(jnp.int32)
            seg_c += (cols >= end).astype(jnp.int32)
        same = seg_r == seg_c
        for h in range(HEADS):
            at, hs = 3 * h * HEAD_DIM, slice(h * HEAD_DIM, (h + 1) * HEAD_DIM)
            q = (acc[:, at : at + HEAD_DIM] + qb[:, hs].astype(F32)).astype(BF)
            key = acc[:, at + HEAD_DIM : at + 2 * HEAD_DIM].astype(BF)
            v = acc[:, at + 2 * HEAD_DIM : at + 3 * HEAD_DIM] + vb[:, hs].astype(F32)
            v = v.astype(BF)
            qkv_o[:, at : at + HEAD_DIM] = q
            qkv_o[:, at + HEAD_DIM : at + 2 * HEAD_DIM] = key
            qkv_o[:, at + 2 * HEAD_DIM : at + 3 * HEAD_DIM] = v
            scores = jnp.where(same, dot_nt(q, key) * scale, -1e30)
            e = jnp.exp(scores - jnp.max(scores, 1, keepdims=True))
            prob = e / jnp.sum(e, 1, keepdims=True)
            prob_o[h] = prob
            ctx_o[:, hs] = dot(prob.astype(BF), v).astype(BF)
        ctx = ctx_o[...]
        for k in range(R):
            for i in range(OP):
                w = ws[k][i * HD : (i + 1) * HD, Q3:]
                scr[:, lanes((r ^ k) * OP + i, HD)] = dot(ctx, w)
        p_own[...] = scr[lanes(c, TH), :]
        p_send[...] = scr[lanes(C - 1 - c, TH), :].astype(BF)

    half32, half16 = ((TQ, D), F32), ((TQ, D), BF)
    xf, vall, qkv, prob, ctx, p_own, p_send = call(
        attention,
        [((T, D), BF), ((R * C, 16, DB), F32), ((T, Q3), BF), ((HEADS, T, T), F32),
         ((T, HD), BF), ((TH, D), F32), ((TH, D), BF)],
        *X, *Y, *A, query_bias.reshape(1, HD), value_bias.reshape(1, HD), doc_lengths,
        scratch=[((T, D), F32)], flops=2 * T * D * (Q3 + HD), smem=(3 * R + 2,),
    )

    def add_split(own, got, a, b, a16, b16):
        s = own[...] + got[...].astype(F32)
        a[...], b[...] = s[:TQ], s[TQ:]
        a16[...], b16[...] = s[:TQ].astype(BF), s[TQ:].astype(BF)

    def all_reduce(a, b, a16, b16):
        got_a, got_b = phop(a16, 0), phop(b16, 1)
        a = a + got_a.astype(F32)
        b = b + got_b.astype(F32)
        return a, b, phop(a.astype(BF), 1), phop(b.astype(BF), 0)

    split_outs = [half32, half32, half16, half16]
    sums_one = all_reduce(*call(add_split, split_outs, p_own, pcol(p_send)))
    ctx_all = [ctx] + [prow(ctx, k) for k in others]

    def wide(vall, i):
        return jnp.concatenate([vall[at, i : i + 1, :] for at in range(R * C)], 1)

    def total(a, b, got_a, got_b):
        return jnp.concatenate(
            [a[...] + got_a[...].astype(F32), b[...] + got_b[...].astype(F32)], 0
        )

    def put_halves(value, a, b, a16, b16):
        a[...], b[...] = value[:TQ], value[TQ:]
        a16[...], b16[...] = value[:TQ].astype(BF), value[TQ:].astype(BF)

    def norm(resid):
        centred = resid - row_mean(resid)
        inv = lax.rsqrt(row_mean(centred * centred) + EPSILON)
        return centred * inv, inv

    def mlp_forward(*refs):
        sums, (xf, vall), rest = refs[:4], refs[4:6], refs[6:]
        bs, ps = rest[:R], rest[R : 2 * R]
        normed_o, inv_o, pre_o, a, b, a16, b16, hid, scr = rest[2 * R :]
        r, c, _ = here()
        resid = total(*sums) + wide(vall, 0) + xf[lanes(c, TH), :].astype(F32)
        normed, inv = norm(resid)
        normed_o[...] = normed
        inv_o[...] = jnp.broadcast_to(inv, inv_o.shape)
        hid[...] = (normed * wide(vall, 1) + wide(vall, 2)).astype(BF)
        acts = []
        for side, (ws, cc) in enumerate(((bs, c), (ps, C - 1 - c))):
            for u in range(NU):
                acc = jnp.zeros((TH, KR), F32)
                for k in range(R):
                    acc += dot(hid[:, lanes(r ^ k, KR)], ws[k][u * KR : (u + 1) * KR, :])
                bias = [
                    vall[pl.ds(zb * C + cc, 1), pl.ds(6 + r, 1), :].reshape(1, DB)
                    for zb in range(u * KR // FW, (u + 1) * KR // FW)
                ]
                pre = acc + jnp.concatenate(bias, 1)
                pre_o[:, side * F8 + u * KR : side * F8 + (u + 1) * KR] = pre
                acts.append((0.5 * pre * (1.0 + lax.erf(pre * math.sqrt(0.5)))).astype(BF))
        for k in range(R):
            acc = jnp.zeros((TH, KR), F32)
            for side, ws in enumerate((bs, ps)):
                for u in range(NU):
                    acc += dot(acts[side * NU + u], ws[k][F8 + u * KR : F8 + (u + 1) * KR, :])
            scr[:, lanes(r ^ k, KR)] = acc
        put_halves(scr[...], a, b, a16, b16)

    normed_one, inv_one, pre, *halves = call(
        mlp_forward,
        [((TH, D), F32), ((TH, DB), F32), ((TH, C * F8), F32)] + split_outs,
        *sums_one, xf, vall, *B, *PB,
        scratch=[((TH, D), BF), ((TH, D), F32)], flops=4 * TH * D * C * F8,
    )
    def pack_c(own, got, out):
        _, c, _ = here()
        out[:, lanes(c, DB)] = own[lanes(c, TH), :]
        out[:, lanes(C - 1 - c, DB)] = got[lanes(c, TH), :]

    cot_in, PB[0] = lax.optimization_barrier((cotangent, PB[0]))
    (cot,) = call(pack_c, [((TH, KR), F32)], cot_in, pcol(cot_in))
    cots = [cot] + [prow(cot, k) for k in others]
    sums_two = all_reduce(*halves)

    W4 = 2 * D + 2 * F8

    def mlp_backward(*refs):
        sums, (normed_r, vall, pre_r), rest = refs[:4], refs[4:7], refs[7:]
        us, bs, ps = rest[:R], rest[R : 2 * R], rest[2 * R : 3 * R]
        lo_own, lo_send, two_o, mine, send, v4, a, b, a16, b16, scr = rest[3 * R :]
        r, c, _ = here()
        hidden = normed_r[...] * wide(vall, 1) + wide(vall, 2)
        mine[:, :D] = hidden.astype(BF)
        send[:, :D] = hidden.astype(BF)
        normed, inv = norm(total(*sums) + wide(vall, 3) + hidden)
        scr[...] = normed * wide(vall, 4) + wide(vall, 5)
        lo_own[...] = scr[:, lanes(r * C + c, DB)]
        lo_send[...] = scr[:, lanes(r * C + C - 1 - c, DB)]
        for k in range(R):
            scr[:, lanes(r ^ k, KR)] = us[k][...]
        u = scr[...]
        scaled = u * wide(vall, 4)
        two = inv * (scaled - row_mean(scaled) - normed * row_mean(scaled * normed))
        two_o[...] = two
        v4[0:1, :] = jnp.sum(u * normed, 0, keepdims=True)
        v4[1:2, :] = jnp.sum(u, 0, keepdims=True)
        v4[2:3, :] = jnp.sum(two, 0, keepdims=True)
        mine[:, D : 2 * D] = two.astype(BF)
        send[:, D : 2 * D] = two.astype(BF)
        pres = []
        for side, (ws, out) in enumerate(((bs, mine), (ps, send))):
            for j in range(NU):
                acc = jnp.zeros((TH, KR), F32)
                for k in range(R):
                    w = ws[k][F8 + j * KR : F8 + (j + 1) * KR, :]
                    acc += dot_nt(mine[:, pl.ds(pl.multiple_of(D + (r ^ k) * KR, KR), KR)], w)
                at = side * F8 + j * KR
                p = pre_r[:, at : at + KR]
                cdf = 0.5 * (1.0 + lax.erf(p * math.sqrt(0.5)))
                slope = cdf + p * jnp.exp(-0.5 * p * p) * (1.0 / math.sqrt(2.0 * math.pi))
                g = acc * slope
                v4[3:4, at : at + KR] = jnp.sum(g, 0, keepdims=True)
                out[:, 2 * D + j * KR : 2 * D + (j + 1) * KR] = (p * cdf).astype(BF)
                g16 = g.astype(BF)
                out[:, 2 * D + F8 + j * KR : 2 * D + F8 + (j + 1) * KR] = g16
                pres.append(g16)
        for k in range(R):
            acc = jnp.zeros((TH, KR), F32)
            for side, ws in enumerate((bs, ps)):
                for j in range(NU):
                    acc += dot_nt(pres[side * NU + j], ws[k][j * KR : (j + 1) * KR, :])
            scr[:, lanes(r ^ k, KR)] = acc
        put_halves(scr[...], a, b, a16, b16)

    lo_own, lo_send, two, mine, send, v4, *halves = call(
        mlp_backward,
        [((TH, DB), F32), ((TH, DB), F32), ((TH, D), F32), ((TH, W4), BF), ((TH, W4), BF),
         ((8, D), F32)] + split_outs,
        *sums_two, normed_one, vall, pre, *cots, *B, *PB,
        scratch=[((TH, D), F32)], flops=4 * TH * D * C * F8,
    )
    sums_three = all_reduce(*halves)
    lo_got = pcol(lo_send)
    core = lax.axis_index("col")
    layer_output = jnp.where(
        core == 0, jnp.concatenate([lo_own, lo_got], 0), jnp.concatenate([lo_got, lo_own], 0)
    )

    def norm_backward(*refs):
        sums, (two, normed_r, inv_r, vall, v4, one_o, pack, vown) = refs[:4], refs[4:]
        grad = two[...] + total(*sums)
        normed = normed_r[...]
        scaled = grad * wide(vall, 1)
        one = scaled - row_mean(scaled) - normed * row_mean(scaled * normed)
        one = inv_r[:, :1] * one
        one_o[...] = one
        pack[:TH] = one.astype(BF)
        vown[...] = jnp.zeros(vown.shape, F32)
        vown[0:3, :] = v4[0:3, :]
        vown[3:4, :] = jnp.sum(grad * normed, 0, keepdims=True)
        vown[4:5, :] = jnp.sum(grad, 0, keepdims=True)
        vown[5:6, :] = jnp.sum(one, 0, keepdims=True)
        vown[6:7, :F8] = v4[3:4, F8:]
        pack[TH:] = vown[...].astype(BF)
        vown[6:7, :F8] = v4[3:4, :F8]

    one, pack, vown = call(
        norm_backward,
        [((TH, D), F32), ((TH + 16, D), BF), ((16, D), F32)],
        *sums_three, two, normed_one, inv_one, vall, v4,
    )
    pack_got = pcol(pack)

    MB = R * ZB + FW * (D // F8)

    def mlp_weights(mine, got, keep, send, scr):
        _, _, z = here()
        for q in range(R):
            cols = slice(q * KR, (q + 1) * KR)
            w = dot_tn(mine[:, cols], mine[:, 2 * D + F8 :])
            w += dot_tn(got[:, cols], got[:, 2 * D + F8 :])
            for zb in range(Z):
                scr[zb, q * ZB : (q + 1) * ZB, :] = w[zb * ZB : (zb + 1) * ZB].astype(BF)
        for j in range(D // F8):
            cols = slice(D + j * F8, D + (j + 1) * F8)
            w = dot_tn(mine[:, 2 * D : 2 * D + F8], mine[:, cols])
            w += dot_tn(got[:, 2 * D : 2 * D + F8], got[:, cols])
            for zb in range(Z):
                at = R * ZB + j * FW
                scr[zb, at : at + FW, :] = w[zb * FW : (zb + 1) * FW].astype(BF)
        for j in range(Z // 2):
            keep[j] = scr[2 * j + (z & 1)]
            send[j] = scr[2 * j + 1 - (z & 1)]

    def halve(keep, got, keep_o, send_o):
        _, _, z = here()
        up = z >> 1
        keep_o[...] = keep[up].astype(F32) + got[up].astype(F32)
        send_o[...] = (keep[1 - up].astype(F32) + got[1 - up].astype(F32)).astype(BF)

    DP = FW * KR // F8

    def mlp_rows(keep, got, *outs):
        r, _, _ = here()
        *outs, scr = outs
        scr[...] = keep[...] + got[...].astype(F32)
        for k in range(R):
            d = r ^ k
            kind = outs[k].dtype
            outs[k][:ZB] = scr[lanes(d, ZB), :].astype(kind)
            per = F8 // KR
            row = R * ZB + lax.div(d, per) * FW
            piece = scr[pl.ds(pl.multiple_of(row, 8), FW), lanes(lax.rem(d, per), KR)]
            for i in range(per):
                outs[k][ZB:, i * KR : (i + 1) * KR] = piece[i * DP : (i + 1) * DP].astype(kind)

    def mlp_place(*refs):
        parts, (up_o, down_o) = refs[:R], refs[R:]
        r, _, _ = here()
        for k in range(R):
            d = r ^ k
            for zb in range(Z):
                up_o[:, lanes(zb * R + d, FW)] = parts[k][:ZB, zb * FW : (zb + 1) * FW].astype(F32)
            for i in range(F8 // KR):
                at = pl.multiple_of(d * FW + i * DP, 8)
                down_o[pl.ds(at, DP), :] = parts[k][ZB:, i * KR : (i + 1) * KR].astype(F32)

    block = ((Z // 2, MB, F8), BF)
    keep, send = call(
        mlp_weights, [block, block], mine, pcol(send),
        scratch=[((Z, MB, F8), BF)], flops=4 * T * D * F8,
    )
    keep, send = call(halve, [((MB, F8), F32), ((MB, F8), BF)], keep, pz(send, 1))
    shapes = [((ZB + DP, F8), F32)] + [((ZB + DP, F8), BF)] * (R - 1)
    parts = call(mlp_rows, shapes, keep, pz(send, 2), scratch=[((MB, F8), F32)])
    parts = [parts[0]] + [prow(parts[k], k) for k in others]
    up_grad, down_grad = call(
        mlp_place, [((ZB, F8 * R), F32), ((FW * R, KR), F32)], *parts
    )

    def attention_backward(*refs):
        ws, cs = refs[:R], refs[R : 2 * R]
        rest = refs[2 * R :]
        pk, pk_got, vown, qkv_r, prob_r, xf, grad_o, own, *outs = rest
        *outs, g1, scr, ow, vs = outs
        r, c, z = here()
        g1[lanes(c, TH), :] = pk[:TH]
        g1[lanes(C - 1 - c, TH), :] = pk_got[:TH]
        acc = jnp.zeros((T, HD), F32)
        for k in range(R):
            for i in range(OP):
                w = ws[k][i * HD : (i + 1) * HD, Q3:]
                acc += dot_nt(g1[:, lanes((r ^ k) * OP + i, HD)], w)
        gctx = acc.astype(BF)
        vs[...] = jnp.zeros(vs.shape, F32)
        for h in range(HEADS):
            at, hs = 3 * h * HEAD_DIM, slice(h * HEAD_DIM, (h + 1) * HEAD_DIM)
            q = qkv_r[:, at : at + HEAD_DIM]
            key = qkv_r[:, at + HEAD_DIM : at + 2 * HEAD_DIM]
            v = qkv_r[:, at + 2 * HEAD_DIM : at + 3 * HEAD_DIM]
            gc = gctx[:, hs]
            prob = prob_r[h]
            gp = dot_nt(gc, v)
            gs = (prob * (gp - jnp.sum(prob * gp, 1, keepdims=True))).astype(BF)
            dq = dot(gs, key) * scale
            dk = dot_tn(gs, q) * scale
            dv = dot_tn(prob.astype(BF), gc)
            vs[10:11, hs] = jnp.sum(dq, 0, keepdims=True)
            vs[11:12, hs] = jnp.sum(dv, 0, keepdims=True)
            grad_o[:, at : at + HEAD_DIM] = dq.astype(BF)
            grad_o[:, at + HEAD_DIM : at + 2 * HEAD_DIM] = dk.astype(BF)
            grad_o[:, at + 2 * HEAD_DIM : at + 3 * HEAD_DIM] = dv.astype(BF)
        grad = grad_o[...]
        for q in range(R):
            scr[q * KR : (q + 1) * KR, :] = dot_tn(xf[:, q * KR : (q + 1) * KR], grad)
        mine = g1[:, lanes(r, KR)]
        for k in range(R):
            ow[r ^ k] = dot_tn(cs[k][...], mine)
        at = lanes(r * C + c, DB)
        vs[0:6, :] = vown[0:6, at] + pk_got[TH:, at].astype(F32)[0:6]
        for zb in range(VB):
            cols = slice(zb * DB, (zb + 1) * DB)
            vs[6 + zb : 7 + zb, :] = vown[6:7, cols] + pk_got[TH:, cols].astype(F32)[6:7]
        for j, out in enumerate([own] + outs):
            d = z ^ j
            kind = out.dtype
            for q in range(R):
                row = pl.multiple_of(q * KR + d * ZB, 8)
                out[q * ZB : (q + 1) * ZB, :Q3] = scr[pl.ds(row, ZB), :].astype(kind)
            for i in range(OP):
                out[i * HD : (i + 1) * HD, Q3:] = ow[d, :, i * HD : (i + 1) * HD].astype(kind)
            out[KR:, :DB] = vs[...].astype(kind)
            out[KR:, DB:] = jnp.zeros((16, Q3 + HD - DB), kind)

    chunk = (KR + 16, Q3 + HD)
    grad_qkv, *parts = call(
        attention_backward,
        [((T, Q3), BF), (chunk, F32)] + [(chunk, BF)] * (Z - 1),
        *A, *ctx_all, pack, pack_got, vown, qkv, prob, xf,
        scratch=[((T, D), BF), ((D, Q3), F32), ((R, HD, KR), F32), ((16, HD), F32)],
        flops=2 * T * D * (2 * HD + Q3),
    )
    parts = [parts[0]] + [pz(parts[j], j) for j in range(1, Z)]

    def input_partial(*refs):
        ws, (grad, one, keep, send, scr) = refs[:R], refs[R:]
        r, c, _ = here()
        for k in range(R):
            scr[...] = dot_nt(grad[...], ws[k][:, :Q3])
            if k == 0:
                scr[lanes(c, TH), :] += one[:, lanes(r, KR)]
            cols = slice(k * DB, (k + 1) * DB)
            keep[:, cols] = scr[:, lanes(c, DB)]
            send[:, cols] = scr[:, lanes(C - 1 - c, DB)].astype(BF)

    keep, send = call(
        input_partial, [((T, R * DB), F32), ((T, R * DB), BF)], *A, grad_qkv, one,
        scratch=[((T, KR), F32)], flops=2 * T * D * Q3,
    )

    def add_rows(keep, got, *outs):
        for k in range(R):
            cols = slice(k * DB, (k + 1) * DB)
            outs[k][...] = (keep[:, cols] + got[:, cols].astype(F32)).astype(outs[k].dtype)

    sums = call(add_rows, [((T, DB), F32)] + [((T, DB), BF)] * (R - 1), keep, pcol(send))
    input_grad = sums[0]
    for k in others:
        input_grad = input_grad + prow(sums[k], k).astype(F32)

    def finish(*refs):
        parts, (ow_o, vec_o, *rest) = refs[:Z], refs[Z:]
        *outs, scr = rest
        r, _, z = here()
        t = parts[0][...]
        for j in range(1, Z):
            t = t + parts[j][...].astype(F32)
        scr[...] = t
        for i in range(OP):
            ow_o[:, i * HD : (i + 1) * HD] = t[i * HD : (i + 1) * HD, Q3:]
        v = scr[KR:, :DB]
        vec_o[...] = pltpu.roll(v, lax.rem(Z - z, Z) * (DB // Z), 1)
        for k in range(R):
            d = r ^ k
            kind = outs[k].dtype
            outs[k][:ZB] = scr[lanes(d, ZB), :Q3].astype(kind)
            outs[k][ZB:, :] = jnp.zeros((16, Q3), kind)
            piece = jnp.zeros((1, DB), F32)
            for zb in range(VB):
                piece += jnp.where(d == zb, v[6 + zb : 7 + zb, :], 0.0)
            outs[k][ZB:, :DB] = jnp.broadcast_to(piece, (16, DB)).astype(kind)

    shapes = [((ZB + 16, Q3), F32)] + [((ZB + 16, Q3), BF)] * (R - 1)
    out_grad, vec_grad, *rows = call(
        finish, [((HD, KR), F32), ((16, DB), F32)] + shapes, *parts,
        scratch=[(chunk, F32)],
    )
    rows = [rows[0]] + [prow(rows[k], k) for k in others]

    def place(*refs):
        parts, (out, upb) = refs[:R], refs[R:]
        r, _, z = here()
        acc = jnp.zeros((8, DB), F32)
        for k in range(R):
            out[:, lanes(r ^ k, Q3)] = parts[k][:ZB].astype(F32)
            acc += jnp.where((r ^ k) == z, parts[k][ZB:, :DB].astype(F32)[:8], 0.0)
        upb[...] = acc

    qkv_grad, upb = call(place, [((ZB, Q3 * R), F32), ((8, DB), F32)], *rows)
    n = DB // Z
    v = [vec_grad[i, :n] for i in range(12)]
    return (
        layer_output, input_grad, qkv_grad, v[10], v[11], out_grad, v[5], v[3], v[4],
        up_grad, upb[0], down_grad, v[2], v[0], v[1],
    )


def matmul(left, right):
    return jnp.dot(left, right, preferred_element_type=jnp.float32)


def matmul_transposed(left, right):
    return lax.dot_general(
        left, right, (((1,), (1,)), ((), ())), preferred_element_type=jnp.float32
    )


def outer_product(left, right):
    return lax.dot_general(
        left, right, (((0,), (0,)), ((), ())), preferred_element_type=jnp.float32
    )


def gelu_value(pre):
    return 0.5 * pre * (1.0 + jax.scipy.special.erf(pre / math.sqrt(2.0)))


def gelu_slope(pre):
    return 0.5 * (1.0 + jax.scipy.special.erf(pre / math.sqrt(2.0))) + pre * jnp.exp(
        -0.5 * pre * pre
    ) / math.sqrt(2.0 * math.pi)


def col_first(features, multiply):
    gathered = lax.all_gather(features, "col", axis=1, tiled=True)
    return (gathered, lax.psum_scatter(multiply(gathered), "row", scatter_dimension=1, tiled=True))


def row_first(features, multiply):
    gathered = lax.all_gather(features, "row", axis=1, tiled=True)
    return (gathered, lax.psum_scatter(multiply(gathered), "col", scatter_dimension=1, tiled=True))


def norm_forward(resid, norm_gain, norm_shift):
    full_width = resid.shape[1] * lax.axis_size("row") * lax.axis_size("col")
    row_total = lax.psum(jnp.sum(resid, 1), ("row", "col"))
    row_mean = row_total / full_width
    centred = resid - row_mean[:, None]
    variance = lax.psum(jnp.sum(centred * centred, 1), ("row", "col")) / full_width
    inv_std = lax.rsqrt(variance + EPSILON)[:, None]
    normed = centred * inv_std
    return (normed * norm_gain + norm_shift, normed, inv_std)


def norm_backward(upstream, normed, inv_std, norm_gain):
    full_width = upstream.shape[1] * lax.axis_size("row") * lax.axis_size("col")
    scaled = upstream * norm_gain
    first_sum, second_sum = lax.psum(
        (jnp.sum(scaled, 1), jnp.sum(scaled * normed, 1)), ("row", "col")
    )
    result = inv_std * (
        scaled - (first_sum / full_width)[:, None] - normed * (second_sum / full_width)[:, None]
    )
    return (result, jnp.sum(upstream * normed, 0), jnp.sum(upstream, 0))


def general_local(
    layer_input,
    doc_lengths,
    qkv_weight,
    query_bias,
    value_bias,
    out_weight,
    out_bias,
    first_gain,
    first_shift,
    up_weight,
    up_bias,
    down_weight,
    down_bias,
    second_gain,
    second_shift,
    cotangent,
):
    bfloat = jnp.bfloat16
    single = jnp.float32
    tokens = layer_input.shape[0]
    heads_here = query_bias.shape[0] // HEAD_DIM
    score_scale = 1.0 / math.sqrt(HEAD_DIM)
    input_near, qkv = col_first(layer_input, lambda gathered: matmul(gathered, qkv_weight))
    qkv = qkv.reshape(tokens, heads_here, 3, HEAD_DIM)
    queries = (qkv[:, :, 0] + query_bias.astype(single).reshape(heads_here, HEAD_DIM)).astype(
        bfloat
    )
    keys = qkv[:, :, 1].astype(bfloat)
    values = (qkv[:, :, 2] + value_bias.astype(single).reshape(heads_here, HEAD_DIM)).astype(bfloat)
    doc_ends = jnp.cumsum(doc_lengths[0])
    position = jnp.arange(tokens)
    segment = jnp.sum((position[:, None] >= doc_ends[None, :]).astype(jnp.int32), 1)
    block_rows = min(512, tokens)
    block_count = tokens // block_rows

    def scores_of():
        raw_scores = (
            jnp.einsum("qhe,khe->hqk", queries, keys, preferred_element_type=single) * score_scale
        )
        same_doc = (segment[:, None] == segment[None, :])[None]
        return (queries, jnp.where(same_doc, raw_scores, -1e30))

    def forward_block(block_index):
        query_rows, scores = scores_of()
        top_score = jnp.max(scores, -1, keepdims=True)
        logsum = top_score + jnp.log(jnp.sum(jnp.exp(scores - top_score), -1, keepdims=True))
        prob_bf = jnp.exp(scores - logsum).astype(bfloat)
        context_rows = jnp.einsum("hqk,khe->qhe", prob_bf, values, preferred_element_type=single)
        return (context_rows.astype(bfloat), logsum[..., 0])

    context_blocks, logsums = lax.map(forward_block, jnp.arange(block_count))
    context = context_blocks.reshape(tokens, heads_here * HEAD_DIM)
    context_near, attention_out = row_first(context, lambda gathered: matmul(gathered, out_weight))
    resid_one = attention_out + out_bias.astype(single) + layer_input.astype(single)
    gain_one = first_gain.astype(single)
    hidden_one, normed_one, inv_one = norm_forward(resid_one, gain_one, first_shift.astype(single))
    hidden_bf = hidden_one.astype(bfloat)
    hidden_near, up_total = col_first(hidden_bf, lambda gathered: matmul(gathered, up_weight))
    pre_act = up_total + up_bias.astype(single)
    activated = gelu_value(pre_act).astype(bfloat)
    active_near, down_out = row_first(activated, lambda gathered: matmul(gathered, down_weight))
    resid_two = down_out + down_bias.astype(single) + hidden_one
    gain_two = second_gain.astype(single)
    layer_output, normed_two, inv_two = norm_forward(
        resid_two, gain_two, second_shift.astype(single)
    )
    grad_two, gain_two_grad, shift_two_grad = norm_backward(
        cotangent, normed_two, inv_two, gain_two
    )
    grad_two_bf = grad_two.astype(bfloat)
    two_near, grad_active = col_first(
        grad_two_bf, lambda gathered: matmul_transposed(gathered, down_weight)
    )
    down_weight_grad = outer_product(active_near, two_near)
    grad_pre = grad_active * gelu_slope(pre_act)
    grad_pre_bf = grad_pre.astype(bfloat)
    pre_near, hidden_back = row_first(
        grad_pre_bf, lambda gathered: matmul_transposed(gathered, up_weight)
    )
    up_weight_grad = outer_product(hidden_near, pre_near)
    grad_hidden = grad_two + hidden_back
    grad_one, gain_one_grad, shift_one_grad = norm_backward(
        grad_hidden, normed_one, inv_one, gain_one
    )
    grad_one_bf = grad_one.astype(bfloat)
    one_near, grad_context = col_first(
        grad_one_bf, lambda gathered: matmul_transposed(gathered, out_weight)
    )
    out_weight_grad = outer_product(context_near, one_near)
    grad_context = grad_context.astype(bfloat).reshape(tokens, heads_here, HEAD_DIM)

    def backward_block(running, block_index):
        query_rows, scores = scores_of()
        probabilities = jnp.exp(scores - logsums[block_index][..., None])
        prob_bf = probabilities.astype(bfloat)
        grad_probs = jnp.einsum("qhe,khe->hqk", grad_context, values, preferred_element_type=single)
        row_dot = jnp.sum(probabilities * grad_probs, -1, keepdims=True)
        grad_scores = (probabilities * (grad_probs - row_dot)).astype(bfloat)
        query_part = (
            jnp.einsum("hqk,khe->qhe", grad_scores, keys, preferred_element_type=single)
            * score_scale
        )
        key_total = (
            running[0]
            + jnp.einsum("hqk,qhe->khe", grad_scores, query_rows, preferred_element_type=single)
            * score_scale
        )
        value_total = running[1] + jnp.einsum(
            "hqk,qhe->khe", prob_bf, grad_context, preferred_element_type=single
        )
        return ((key_total, value_total), query_part)

    zero_state = jnp.zeros((tokens, heads_here, HEAD_DIM), single)
    (key_grad, value_grad), query_parts = lax.scan(
        backward_block, (zero_state, zero_state), jnp.arange(block_count)
    )
    query_grad = query_parts.reshape(tokens, heads_here, HEAD_DIM)
    grad_qkv = (
        jnp.stack([query_grad, key_grad, value_grad], 2)
        .reshape(tokens, heads_here * 3 * HEAD_DIM)
        .astype(bfloat)
    )
    qkv_near, input_back = row_first(
        grad_qkv, lambda gathered: matmul_transposed(gathered, qkv_weight)
    )
    qkv_weight_grad = outer_product(input_near, qkv_near)
    input_grad = grad_one + input_back
    summed = (
        lax.psum_scatter(
            qkv_weight_grad.astype(jnp.bfloat16), "dp", scatter_dimension=0, tiled=True
        ).astype(jnp.float32),
        lax.psum_scatter(
            jnp.sum(query_grad, 0).reshape(-1).astype(jnp.bfloat16),
            "dp",
            scatter_dimension=0,
            tiled=True,
        ).astype(jnp.float32),
        lax.psum_scatter(
            jnp.sum(value_grad, 0).reshape(-1).astype(jnp.bfloat16),
            "dp",
            scatter_dimension=0,
            tiled=True,
        ).astype(jnp.float32),
        lax.psum_scatter(
            out_weight_grad.astype(jnp.bfloat16), "dp", scatter_dimension=0, tiled=True
        ).astype(jnp.float32),
        lax.psum_scatter(
            jnp.sum(grad_one, 0).astype(jnp.bfloat16), "dp", scatter_dimension=0, tiled=True
        ).astype(jnp.float32),
        lax.psum_scatter(
            gain_one_grad.astype(jnp.bfloat16), "dp", scatter_dimension=0, tiled=True
        ).astype(jnp.float32),
        lax.psum_scatter(
            shift_one_grad.astype(jnp.bfloat16), "dp", scatter_dimension=0, tiled=True
        ).astype(jnp.float32),
        lax.psum_scatter(
            up_weight_grad.astype(jnp.bfloat16), "dp", scatter_dimension=0, tiled=True
        ).astype(jnp.float32),
        lax.psum_scatter(
            jnp.sum(grad_pre, 0).astype(jnp.bfloat16), "dp", scatter_dimension=0, tiled=True
        ).astype(jnp.float32),
        lax.psum_scatter(
            down_weight_grad.astype(jnp.bfloat16), "dp", scatter_dimension=0, tiled=True
        ).astype(jnp.float32),
        lax.psum_scatter(
            jnp.sum(grad_two, 0).astype(jnp.bfloat16), "dp", scatter_dimension=0, tiled=True
        ).astype(jnp.float32),
        lax.psum_scatter(
            gain_two_grad.astype(jnp.bfloat16), "dp", scatter_dimension=0, tiled=True
        ).astype(jnp.float32),
        lax.psum_scatter(
            shift_two_grad.astype(jnp.bfloat16), "dp", scatter_dimension=0, tiled=True
        ).astype(jnp.float32),
    )
    return (layer_output, input_grad) + tuple(summed)


def solution(mesh):
    axes = mesh.shape
    square = axes["col"] == 2 and axes["row"] == 4 and axes["dp"] == 4
    return jax.shard_map(
        fast_local if square else general_local,
        mesh=mesh,
        in_specs=(
            P("dp", ("row", "col")),
            P("dp", None),
            P("row", "col"),
            P(("col", "row")),
            P(("col", "row")),
            P("col", "row"),
            P(("row", "col")),
            P(("row", "col")),
            P(("row", "col")),
            P("row", "col"),
            P(("col", "row")),
            P("col", "row"),
            P(("row", "col")),
            P(("row", "col")),
            P(("row", "col")),
            P("dp", ("row", "col")),
        ),
        out_specs=(
            P("dp", ("row", "col")),
            P("dp", ("row", "col")),
            P(("row", "dp"), "col"),
            P(("col", "row", "dp")),
            P(("col", "row", "dp")),
            P(("col", "dp"), "row"),
            P(("row", "col", "dp")),
            P(("row", "col", "dp")),
            P(("row", "col", "dp")),
            P(("row", "dp"), "col"),
            P(("col", "row", "dp")),
            P(("col", "dp"), "row"),
            P(("row", "col", "dp")),
            P(("row", "col", "dp")),
            P(("row", "col", "dp")),
        ),
        check_vma=False,
    )
```
